768 devices in a mesh: band: 96 (over z, y), lev: 8 (over x, core).
Axes of the slice: x: 4, y: 8, z: 12, core: 2. Of those that a mesh axis runs over, the one named last changes fastest.
Arguments:
- spectra: bfloat16 [1344, 2, 120, 1280], P('band', None, 'lev'), may hold values from -6 to 6
- legendre: bfloat16 [1344, 1280, 192], P('band'), may hold values from -0.15625 to 0.15625
- slot_wave: int32 [1344], replicated, may hold values from -1 to 1279, as said below
- row_points: int32 [192], replicated, may hold values from 20 to 5136, as said below
- gauss_weight: float32 [192], replicated, may hold values from 0.5 to 2
- layer_depth: float32 [24], replicated, may hold values from 0.1 to 1
- mode_speed: float32 [120], P('lev'), may hold values from 0.5 to 8
Outputs:
- advanced: float32 [1344, 2, 120, 1280], P('band', None, 'lev')
The draws below stay inside these ranges and needn't reach their ends.
Inputs may be any that keep to these rules, and one draw needn't show every extreme that they name: `slot_wave`: every wavenumber 0 to 1279 stands in exactly one slot. Slots 2k and 2k + 1 of one index of band hold a pair m and 1279 - m, or are both empty. `row_points`: rows 2k and 2k + 1 have 20 + 4 i and 20 + 4 (1279 - i) points for some i in 0 to 1279, in either order, so that together they have 4 * 1279 + 40 points.
All inputs are finite; a program needn't handle non-finite values.
Results may differ from the reference program's by a relative error of at most 0.0043.
Values may be sent and summed in bfloat16 or wider, within the bound.
A program may use at most 64 MiB of HBM per device.

```python
import math
import jax
import jax.numpy as jnp
from jax import lax

TRUNC = 1279
FIELDS = 5
LEVELS = 24
NDEG = 1280
FLD = 120
SLOTS = 1344
NLAT = 192
NLON_MAX = 5136
N_BAND = 96


def draw_slot_wave(key, part):
    pair_count = (TRUNC + 1) // 2
    slot_count = 2 * ((pair_count + N_BAND - 1) // N_BAND)
    shuffled = jax.random.permutation(key, pair_count).astype(jnp.int32)
    swapped = jax.random.randint(jax.random.fold_in(key, 7), (pair_count,), 0, 2)
    high_wave = TRUNC - shuffled
    first_wave = jnp.where(swapped == 1, high_wave, shuffled)
    second = jnp.where(swapped == 1, shuffled, high_wave)
    position = jnp.arange(pair_count, dtype=jnp.int32)
    device = position % N_BAND
    slot_at = device * slot_count + 2 * (position // N_BAND)
    wave_table = jnp.full((slot_count * N_BAND,), -1, jnp.int32)
    wave_table = wave_table.at[slot_at].set(first_wave).at[slot_at + 1].set(second)
    return wave_table


def draw_row_points(key, part):
    chosen = jax.random.randint(key, (N_BAND,), 0, TRUNC + 1).astype(jnp.int32)
    chosen = chosen.at[0].set(TRUNC)
    swapped = jax.random.randint(jax.random.fold_in(key, 3), (N_BAND,), 0, 2)
    north_pts = 20 + 4 * chosen
    south_pts = 20 + 4 * (TRUNC - chosen)
    first_row = jnp.where(swapped == 1, south_pts, north_pts)
    second = jnp.where(swapped == 1, north_pts, south_pts)
    return jnp.stack([first_row, second], axis=1).reshape(2 * N_BAND).astype(jnp.int32)


def steps_of(stream_key, dims, split, smallest, top_value):
    def one(dim, blocks):
        heights = jax.random.uniform(jax.random.fold_in(jax.random.fold_in(stream_key, 6), dim), (blocks,), jnp.float32, smallest / len(split), top_value / len(split))
        return jnp.repeat(jnp.exp(heights), dims[dim] // blocks).reshape((-1,) + (1,) * (len(dims) - dim - 1))

    loudness = one(*split[0])
    for cut in split[1:]:
        loudness = loudness * one(*cut)
    return loudness


def centred(stream_key, dims, spread, limit, shards=(), kind=jnp.bfloat16):
    loudness = steps_of(stream_key, dims, shards, -0.22, 0.18) if shards else 1.0
    result = jax.random.normal(stream_key, dims, jnp.float32) * spread * loudness
    return jnp.minimum(jnp.maximum(result, -limit), limit).astype(kind)


def setup_inputs(seed: int = 0) -> dict:
    keys = jax.random.split(jax.random.key(seed), 8)
    spectra = centred(keys[0], (SLOTS, 2, FLD, NDEG), 1.0, 6.0, ((0, 96), (2, 8)))
    legendre = centred(keys[1], (SLOTS, NDEG, NLAT), NDEG ** -0.5, 0.15625, ((0, 96),))
    slot_wave = draw_slot_wave(jax.random.fold_in(keys[7], 71), 0)
    row_points = draw_row_points(jax.random.fold_in(keys[7], 71), 0)
    gauss_weight = jnp.clip(jnp.exp(jax.random.uniform(keys[4], (NLAT,), jnp.float32, math.log(0.5), math.log(2.0))), 0.5, 2.0)
    layer_depth = jnp.clip(jnp.exp(jax.random.uniform(keys[5], (LEVELS,), jnp.float32, math.log(0.1), math.log(1.0))), 0.1, 1.0)
    mode_speed = jnp.clip(jnp.exp(math.log(8.0) - 2.7725887 * jax.random.uniform(keys[6], (FLD,), jnp.float32) ** steps_of(keys[6], (FLD,), ((0, 8),), -0.2, 0.2)), 0.5, 8.0)
    return dict(spectra=spectra, legendre=legendre, slot_wave=slot_wave, row_points=row_points, gauss_weight=gauss_weight, layer_depth=layer_depth, mode_speed=mode_speed)


precise = lax.Precision.HIGHEST
time_step = 1.0

def make_basis(wave_table, row_len, column, inside):
    wave_num = jnp.maximum(wave_table, 0)[:, None]
    residue = wave_num * column[None, :] % row_len[None, :]
    row_float = row_len.astype(jnp.float32)[None, :]
    phase_angle = residue.astype(jnp.float32) * (2.0 * math.pi / row_float)
    active = (wave_table[:, None] >= 0) & (2 * wave_table[:, None] <= row_len[None, :] - 1) & inside[None, :]
    norm_scale = jnp.where(active, 1.0 / jnp.sqrt(row_float), jnp.zeros((), jnp.float32))
    return jnp.stack([jnp.cos(phase_angle) * norm_scale, -jnp.sin(phase_angle) * norm_scale]).astype(jnp.bfloat16)

def grid_terms(grid_vals, layer_depth):
    width = grid_vals.shape[1]
    stacked = grid_vals.reshape(FIELDS, LEVELS, width)
    wind_u = stacked[0]
    wind_v = stacked[1]
    temper = stacked[2]
    humid = stacked[3]
    ozone_mix = stacked[4]
    level_ids = jnp.arange(LEVELS, dtype=jnp.int32)
    tri_ones = (level_ids[None, :] >= level_ids[:, None]).astype(jnp.float32) * layer_depth[None, :]
    geopotential = jnp.dot(tri_ones, temper, precision=precise)
    energy = 0.5 * (wind_u * wind_u + wind_v * wind_v) + geopotential
    outputs = jnp.stack([wind_u * temper, wind_v * temper, wind_u * humid, wind_v * ozone_mix, energy])
    return outputs.reshape(FIELDS * LEVELS, width).astype(jnp.bfloat16)

def reference(spectra, legendre, slot_wave, row_points, gauss_weight, layer_depth, mode_speed):
    degree = jnp.arange(NDEG, dtype=jnp.int32)
    live_mask = (slot_wave[:, None] >= 0) & (degree[None, :] >= slot_wave[:, None])
    masked = jnp.where(live_mask[:, None, None, :], spectra, jnp.zeros((), spectra.dtype))

    def inverse_slot(operands):
        coeffs, table = operands
        product = jnp.einsum('cfn,nr->rcf', coeffs.astype(jnp.float32), table.astype(jnp.float32), precision=precise)
        return product.astype(jnp.bfloat16)
    fourier = jnp.transpose(lax.map(inverse_slot, (masked, legendre)), (1, 0, 2, 3))
    weight_mult = (jnp.where(slot_wave == 0, 1.0, 2.0) * (slot_wave >= 0)).astype(jnp.float32)
    column = jnp.arange(NLON_MAX, dtype=jnp.int32)

    def one_row(operands):
        coeffs, row_count, row_weight = operands
        row_len = jnp.full((NLON_MAX,), row_count, jnp.int32)
        basis_table = make_basis(slot_wave, row_len, column, column < row_count).astype(jnp.float32)
        scaled = coeffs.astype(jnp.float32) * weight_mult[:, None, None]
        grid_vals = jnp.einsum('scf,csp->fp', scaled, basis_table, precision=precise)
        tendency = grid_terms(grid_vals, layer_depth).astype(jnp.float32)
        analysed = jnp.einsum('fp,csp->scf', tendency, basis_table, precision=precise)
        return (analysed * row_weight).astype(jnp.bfloat16)
    returned = lax.map(one_row, (fourier, row_points, gauss_weight))

    def forward_slot(operands):
        coeffs, table = operands
        return jnp.einsum('rcf,nr->cfn', coeffs.astype(jnp.float32), table.astype(jnp.float32), precision=precise)
    tendency_spec = lax.map(forward_slot, (jnp.transpose(returned, (1, 0, 2, 3)), legendre))
    helm_factor = (degree * (degree + 1)).astype(jnp.float32) / float(TRUNC * (TRUNC + 1))
    denominator = 1.0 + time_step * time_step * helm_factor[None, None, None, :] * mode_speed[None, None, :, None]
    advanced = (masked.astype(jnp.float32) + time_step * tendency_spec) / denominator
    return jnp.where(live_mask[:, None, None, :], advanced, jnp.zeros((), advanced.dtype))
```

```python
import functools

import jax
import jax.numpy as jnp
from jax import lax
from jax.experimental import pallas as pl
from jax.experimental.pallas import tpu as pltpu
from jax.sharding import PartitionSpec as P

TRUNC = 1279
FIELDS = 5
LEVELS = 24
FPAD = 16
LANES = 128
CHUNKS = 6
POINTS = CHUNKS * LANES
IMAGES = 8
JPAD = 8
F32 = jnp.float32
BF16 = jnp.bfloat16
I32 = jnp.int32
MESH = pl.DeviceIdType.MESH
NT = (((1,), (1,)), ((), ()))


def dot(a, b):
    return jnp.dot(a, b, preferred_element_type=F32)


def iota(shape, dim):
    return lax.broadcasted_iota(I32, shape, dim)


def lev_of_chunk(chunk):
    return chunk + chunk // 3


def quarter_turn_pair(quarters):
    nearest = jnp.round(quarters)
    u = quarters - nearest
    turn = nearest.astype(I32)
    u2 = u * u
    sin_u = u * (1.5707963 + u2 * (-0.6459640 + u2 * (0.07969087 + u2 * (-0.0046737664 + u2 * 0.00015148))))
    cos_u = 1.0 + u2 * (-1.2337005 + u2 * (0.25366950 + u2 * (-0.020863453 + u2 * 0.00091814)))
    odd = (turn & 1) == 1
    cos_v = jnp.where(odd, sin_u, cos_u)
    sin_v = jnp.where(odd, cos_u, sin_u)
    cos_v = jnp.where(((turn + 1) & 2) == 2, -cos_v, cos_v)
    sin_v = jnp.where((turn & 2) == 2, -sin_v, sin_v)
    return cos_v, sin_v


def base_points(p, first_points, second_points):
    first_count = first_points // 8 + 1
    second = p >= first_count
    index = jnp.where(second, p - first_count, p)
    length = jnp.where(second, second_points, first_points)
    return second, index, length, 8 * index <= length


def turn(wave, k):
    step = (jnp.maximum(wave, 0) * k) & 3
    real = jnp.where(step == 0, 1.0, jnp.where(step == 2, -1.0, 0.0))
    imag = jnp.where(step == 1, 1.0, jnp.where(step == 3, -1.0, 0.0))
    return real, imag


def round_kernel(
    nb,
    nl,
    wave_s,
    points_s,
    gauss_s,
    layer_s,
    wave_ref,
    spec_ref,
    leg_hbm,
    out_ref,
    leg_v,
    mix,
    fsend32,
    fsend,
    frecv,
    cos_v,
    sin_v,
    coef,
    rep,
    cos_w,
    sin_w,
    gsend,
    grecv,
    terms32,
    tsend,
    trecv,
    sums,
    diffs,
    ztab,
    back,
    bsend,
    leg_sem,
    send_sem,
    recv_sem,
):
    slots = leg_v.shape[0]
    pairs = slots // 2
    ndeg = leg_v.shape[2]
    nfld = spec_ref.shape[1]
    half = nb * JPAD
    qblock = min(16, nb)
    rows = qblock * JPAD
    blocks = nb // qblock
    band = lax.axis_index("band")
    lev = lax.axis_index("lev")

    copies = [pltpu.make_async_copy(leg_hbm.at[s], leg_v.at[s], leg_sem.at[s]) for s in range(slots)]
    for copy in copies:
        copy.start()

    barrier = pltpu.get_barrier_semaphore()

    @pl.loop(1, nb)
    def _(step):
        pl.semaphore_signal(barrier, inc=1, device_id=(lax.rem(band + step, nb), lev), device_id_type=MESH)

    @pl.loop(1, nl)
    def _(step):
        pl.semaphore_signal(barrier, inc=1, device_id=(band, lax.rem(lev + step, nl)), device_id_type=MESH)

    fsend32[...] = jnp.zeros_like(fsend32)
    degree = iota((2 * FPAD, ndeg), 1)
    blank = jnp.zeros((4 * FPAD, ndeg), BF16)
    fill = jnp.zeros((2 * FPAD - 2 * nfld, ndeg), BF16)
    second_lane = (iota((nb, LANES), 1) // (2 * FPAD)) % 2 == 1
    for j in range(pairs):
        parts = []
        for parity in range(2):
            s = 2 * j + parity
            wave = wave_s[band * slots + s]
            values = spec_ref[s].reshape(2 * nfld, ndeg)
            values = jnp.concatenate([values, fill], axis=0)
            first_degree = jnp.where(wave < 0, ndeg, wave)
            values = jnp.where(degree >= first_degree, values.astype(F32), 0.0).astype(BF16)
            whole = [values, values, blank] if parity == 0 else [blank, values, values]
            copies[s].wait()
            parts.append(
                lax.dot_general(leg_v[s], jnp.concatenate(whole, axis=0), NT, preferred_element_type=F32)
            )
        mix[...] = parts[0] + parts[1]
        first = mix[pl.ds(0, nb, stride=2), :]
        other = mix[pl.ds(1, nb, stride=2), :]
        fsend32[:, j, :] = jnp.where(second_lane, other, first)

    @pl.loop(0, blocks)
    def _(b):
        fsend[pl.ds(b * qblock, qblock)] = fsend32[pl.ds(b * qblock, qblock)].astype(BF16)

    pl.semaphore_wait(barrier, nb - 1 + nl - 1)

    @pl.loop(1, nb)
    def _(step):
        peer = lax.rem(band + step, nb)
        pltpu.make_async_remote_copy(
            src_ref=fsend.at[peer],
            dst_ref=frecv.at[band],
            send_sem=send_sem.at[0],
            recv_sem=recv_sem.at[0],
            device_id=(peer, lev),
            device_id_type=MESH,
        ).start()

    frecv[band] = fsend[band]

    first_points = points_s[2 * band]
    second_points = points_s[2 * band + 1]

    @pl.loop(0, POINTS // 16)
    def _(i):
        p = i * 16 + iota((16, LANES), 0)
        _, index, length, valid = base_points(p, first_points, second_points)
        length = length.astype(F32)
        inverse = 1.0 / length
        index = index.astype(F32)
        scale = 1.0 / jnp.sqrt(length)
        limit = jnp.where(valid, length - 1.0, -1.0)
        for lane in range(2 * half // rows):
            cut = pl.ds(lane * rows, rows)
            wave = wave_ref[:, cut].astype(F32)
            if rows < LANES:
                place = [v[:, :rows] for v in (index, inverse, length, scale, limit)]
            else:
                place = [index, inverse, length, scale, limit]
            at, inv, size, height, top = place
            product = wave * at
            residue = product - jnp.floor(product * inv) * size
            cos_p, sin_p = quarter_turn_pair(residue * (4.0 * inv))
            height = jnp.where((2.0 * wave <= top) & (wave >= 0.0), height, 0.0)
            cos_v[pl.ds(i * 16, 16), cut] = (cos_p * height).astype(BF16)
            sin_v[pl.ds(i * 16, 16), cut] = (sin_p * height).astype(BF16)

    lane_k = iota((rows, LANES), 1)
    flip = jnp.where((lane_k // 4) % 2 == 0, -1.0, 1.0)
    for b in range(2 * blocks):
        cut = pl.ds(b * rows, rows)
        column = jnp.broadcast_to(wave_ref[:, cut].astype(F32), (LANES, rows)).T.astype(I32)
        real, imag = turn(column, lane_k % 4)
        mult = jnp.where(column < 0, 0.0, jnp.where(column == 0, 1.0, 2.0))
        coef[0, cut] = real * mult
        coef[1, cut] = -imag * mult
        coef[2, cut] = flip * real * mult
        coef[3, cut] = flip * imag * mult
        row_re, row_im = turn(jnp.broadcast_to(wave_ref[:, cut], (4, rows)), iota((4, rows), 0))
        ztab[pl.ds(0, 4), cut] = row_re
        ztab[pl.ds(4, 4), cut] = -row_im
    source = iota((LANES, 2 * LANES), 0)
    target = iota((LANES, 2 * LANES), 1)
    wanted = (target // LANES) * (2 * FPAD) + (target % LANES) // IMAGES * 2
    for parity in range(2):
        for component in range(2):
            hit = source == wanted + parity * 4 * FPAD + component
            rep[2 * parity + component] = jnp.where(hit, 1.0, 0.0).astype(BF16)

    pltpu.make_async_copy(frecv.at[pl.ds(0, nb - 1)], frecv.at[pl.ds(0, nb - 1)], recv_sem.at[0]).wait()

    @pl.loop(0, blocks)
    def _(b):
        block = frecv[pl.ds(b * qblock, qblock)].reshape(rows, LANES)
        for parity in range(2):
            cut = pl.ds(pl.multiple_of(parity * half + b * rows, rows), rows)
            part_re = dot(block, rep[2 * parity])
            part_im = dot(block, rep[2 * parity + 1])
            for row in range(2):
                lanes = slice(row * LANES, row * LANES + LANES)
                re, im = part_re[:, lanes], part_im[:, lanes]
                cos_w[cut, lanes] = (coef[0, cut] * re + coef[1, cut] * im).astype(BF16)
                sin_w[cut, lanes] = (coef[2, cut] * im + coef[3, cut] * re).astype(BF16)

    @pl.loop(0, CHUNKS // 2)
    def _(c):
        cut = pl.ds(pl.multiple_of(c * 2 * LANES, 2 * LANES), 2 * LANES)
        values = dot(cos_v[cut, :], cos_w[...]) + dot(sin_v[cut, :], sin_w[...])
        for part in range(2):
            here = slice(part * LANES, part * LANES + LANES)
            p = (2 * c + part) * LANES + iota((LANES, LANES), 0)
            second, _, _, _ = base_points(p, first_points, second_points)
            chosen = jnp.where(second, values[here, LANES:], values[here, :LANES])
            gsend[2 * c + part] = chosen.T.astype(BF16).reshape(FPAD, IMAGES, LANES)

    for chunk in range(CHUNKS):
        target_lev = lev_of_chunk(chunk)

        @pl.when(lev != target_lev)
        def _():
            pltpu.make_async_remote_copy(
                src_ref=gsend.at[chunk],
                dst_ref=grecv.at[lev],
                send_sem=send_sem.at[1],
                recv_sem=recv_sem.at[1],
                device_id=(band, target_lev),
                device_id_type=MESH,
            ).start()

        @pl.when(lev == target_lev)
        def _():
            grecv[lev] = gsend[chunk]

    works = lax.rem(lev, 4) != 3

    @pl.when(works)
    def _():
        pltpu.make_async_copy(grecv.at[pl.ds(0, nl - 1)], grecv.at[pl.ds(0, nl - 1)], recv_sem.at[1]).wait()
        chunk = lev - lev // 4
        terms32[...] = jnp.zeros_like(terms32)

        def get(field, level):
            f = field * LEVELS + level
            return grecv[f // nfld, f % nfld].astype(F32)

        def put(field, level, value):
            f = field * LEVELS + level
            terms32[f // nfld, :, f % nfld, :] = value

        total = jnp.zeros((IMAGES, LANES), F32)
        for level in reversed(range(LEVELS)):
            wind_u, wind_v, temper = get(0, level), get(1, level), get(2, level)
            total = total + layer_s[level] * temper
            put(0, level, wind_u * temper)
            put(1, level, wind_v * temper)
            put(2, level, wind_u * get(3, level))
            put(3, level, wind_v * get(4, level))
            put(4, level, 0.5 * (wind_u * wind_u + wind_v * wind_v) + total)
        for target_lev in range(nl):
            tsend[target_lev] = terms32[target_lev].reshape(LANES, LANES).astype(BF16)

        @pl.loop(1, nl)
        def _(step):
            peer = lax.rem(lev + step, nl)
            pltpu.make_async_remote_copy(
                src_ref=tsend.at[peer],
                dst_ref=trecv.at[chunk],
                send_sem=send_sem.at[2],
                recv_sem=recv_sem.at[2],
                device_id=(band, peer),
                device_id_type=MESH,
            ).start()

        trecv[chunk] = tsend[lev]
        pltpu.make_async_copy(
            trecv.at[pl.ds(0, CHUNKS - 1)], trecv.at[pl.ds(0, CHUNKS - 1)], recv_sem.at[2]
        ).wait()

    @pl.when(jnp.logical_not(works))
    def _():
        pltpu.make_async_copy(trecv, trecv, recv_sem.at[2]).wait()

    for chunk in range(CHUNKS):
        p = chunk * LANES + iota((1, LANES), 1)
        second, index, length, valid = base_points(p, first_points, second_points)
        alone = (index == 0) | (8 * index == length)
        keep = jnp.where(valid, jnp.where(alone, 0.5, 1.0), 0.0)
        pieces = trecv[chunk].astype(F32)
        plus, minus = pieces[: 4 * FPAD], pieces[4 * FPAD :]
        lanes = slice(chunk * LANES, chunk * LANES + LANES)
        for row in range(2):
            kept = jnp.where(second, keep, 0.0) if row else jnp.where(second, 0.0, keep)
            to = slice(row * 4 * FPAD, (row + 1) * 4 * FPAD)
            sums[to, lanes] = ((plus + minus) * kept).astype(BF16)
            diffs[to, lanes] = ((plus - minus) * kept).astype(BF16)

    for b in range(blocks):
        for parity in range(2):
            cut = pl.ds(parity * half + b * rows, rows)
            cos_z = dot(sums[...], cos_v[:, cut])
            sin_z = dot(diffs[...], sin_v[:, cut])
            for row in range(2):
                re = jnp.zeros((FPAD, rows), F32)
                im = jnp.zeros((FPAD, rows), F32)
                for k in range(4):
                    at = (row * 4 + k) * FPAD
                    zr, zi = ztab[pl.ds(k, 1), cut], ztab[pl.ds(4 + k, 1), cut]
                    cz, sz = cos_z[at : at + FPAD], sin_z[at : at + FPAD]
                    re = re + zr * cz + zi * sz
                    im = im + zi * cz - zr * sz
                weight = gauss_s[2 * band + row]
                at = parity * 4 * FPAD + row * 2 * FPAD
                back[pl.ds(at, FPAD, stride=2), :] = re * weight
                back[pl.ds(at + 1, FPAD, stride=2), :] = im * weight
        bsend[pl.ds(b * qblock, qblock)] = back[...].T.astype(BF16).reshape(qblock, JPAD, LANES)

    @pl.loop(1, nb)
    def _(step):
        peer = lax.rem(band + step, nb)
        pltpu.make_async_remote_copy(
            src_ref=bsend.at[peer],
            dst_ref=out_ref.at[band],
            send_sem=send_sem.at[3],
            recv_sem=recv_sem.at[3],
            device_id=(peer, lev),
            device_id_type=MESH,
        ).start()

    out_ref[band] = bsend[band]
    pltpu.make_async_copy(out_ref.at[pl.ds(0, nb - 1)], out_ref.at[pl.ds(0, nb - 1)], recv_sem.at[3]).wait()

    pltpu.make_async_copy(fsend.at[pl.ds(0, nb - 1)], fsend.at[pl.ds(0, nb - 1)], send_sem.at[0]).wait()
    pltpu.make_async_copy(bsend.at[pl.ds(0, nb - 1)], bsend.at[pl.ds(0, nb - 1)], send_sem.at[3]).wait()

    @pl.when(works)
    def _():
        pltpu.make_async_copy(gsend.at[pl.ds(0, CHUNKS - 1)], gsend.at[pl.ds(0, CHUNKS - 1)], send_sem.at[1]).wait()
        pltpu.make_async_copy(tsend.at[pl.ds(0, nl - 1)], tsend.at[pl.ds(0, nl - 1)], send_sem.at[2]).wait()

    @pl.when(jnp.logical_not(works))
    def _():
        pltpu.make_async_copy(gsend, gsend, send_sem.at[1]).wait()


def update_kernel(nb, wave_s, wide_ref, arrived_ref, spec_ref, leg_ref, inverse_ref, out_ref, wide, mix, left):
    j = pl.program_id(0)
    band = lax.axis_index("band")
    ndeg = leg_ref.shape[2]
    nfld = spec_ref.shape[1]
    pairs = pl.num_programs(0)

    @pl.when(j == 0)
    def _():
        wide[...] = arrived_ref[...].astype(F32)

    mine = wide[:, j, :]
    mix[pl.ds(0, nb, stride=2), :] = mine
    mix[pl.ds(1, nb, stride=2), :] = mine
    nlat = mix.shape[0]
    fits = (iota((nlat, LANES), 0) % 2) == (iota((nlat, LANES), 1) // (2 * FPAD)) % 2
    turned = jnp.where(fits, mix[...], 0.0).T
    degree = iota((2 * nfld, ndeg), 1)
    for parity in range(2):
        at = parity * 4 * FPAD
        both = (turned[at : at + 2 * FPAD] + turned[at + 2 * FPAD : at + 4 * FPAD]).astype(BF16)
        tendency = dot(both, leg_ref[parity])[: 2 * nfld]
        wave = wave_s[band * 2 * pairs + 2 * j + parity]
        first_degree = jnp.where(wave < 0, ndeg, wave)
        values = spec_ref[parity].reshape(2 * nfld, ndeg).astype(F32)
        advanced = (values + tendency) * inverse_ref[...]
        advanced = jnp.where(degree >= first_degree, advanced, 0.0)
        out_ref[parity] = advanced.reshape(nfld, 2, ndeg)


def shards(spectra, legendre, slot_wave, row_points, gauss_weight, layer_depth, mode_speed):
    slots, _, nfld, ndeg = spectra.shape
    nb = lax.axis_size("band")
    nl = lax.axis_size("lev")
    nlat = legendre.shape[2]
    pairs = slots // 2
    half = nb * JPAD
    rows = min(16, nb) * JPAD
    wave = slot_wave.reshape(nb, pairs, 2).transpose(2, 0, 1)
    wave = jnp.pad(wave, ((0, 0), (0, 0), (0, JPAD - pairs)), constant_values=-1).reshape(1, 2 * half)
    spec_rows = spectra.transpose(0, 2, 1, 3)
    leg_rows = legendre.transpose(0, 2, 1)
    smem = pl.BlockSpec(memory_space=pltpu.SMEM)
    vmem = pl.BlockSpec(memory_space=pltpu.VMEM)
    arrived = pl.pallas_call(
        functools.partial(round_kernel, nb, nl),
        out_shape=jax.ShapeDtypeStruct((nb, JPAD, LANES), BF16),
        in_specs=[smem] * 4 + [vmem, vmem, pl.BlockSpec(memory_space=pl.ANY)],
        out_specs=vmem,
        scratch_shapes=[
            pltpu.VMEM((slots, nlat, ndeg), BF16),
            pltpu.VMEM((nlat, LANES), F32),
            pltpu.VMEM((nb, JPAD, LANES), F32),
            pltpu.VMEM((nb, JPAD, LANES), BF16),
            pltpu.VMEM((nb, JPAD, LANES), BF16),
            pltpu.VMEM((POINTS, 2 * half), BF16),
            pltpu.VMEM((POINTS, 2 * half), BF16),
            pltpu.VMEM((4, 2 * half, LANES), F32),
            pltpu.VMEM((4, LANES, 2 * LANES), BF16),
            pltpu.VMEM((2 * half, 2 * LANES), BF16),
            pltpu.VMEM((2 * half, 2 * LANES), BF16),
            pltpu.VMEM((CHUNKS, FPAD, IMAGES, LANES), BF16),
            pltpu.VMEM((nl, FPAD, IMAGES, LANES), BF16),
            pltpu.VMEM((nl, IMAGES, FPAD, LANES), F32),
            pltpu.VMEM((nl, LANES, LANES), BF16),
            pltpu.VMEM((CHUNKS, LANES, LANES), BF16),
            pltpu.VMEM((LANES, POINTS), BF16),
            pltpu.VMEM((LANES, POINTS), BF16),
            pltpu.VMEM((8, 2 * half), F32),
            pltpu.VMEM((LANES, rows), F32),
            pltpu.VMEM((nb, JPAD, LANES), BF16),
            pltpu.SemaphoreType.DMA((slots,)),
            pltpu.SemaphoreType.DMA((4,)),
            pltpu.SemaphoreType.DMA((4,)),
        ],
        compiler_params=pltpu.CompilerParams(
            collective_id=0, has_side_effects=True, vmem_limit_bytes=56 * 1024 * 1024
        ),
    )(slot_wave, row_points, gauss_weight, layer_depth, wave, spec_rows, leg_rows)

    degree = jnp.arange(ndeg, dtype=I32)
    helm = (degree * (degree + 1)).astype(F32) / float(TRUNC * (TRUNC + 1))
    inverse = 1.0 / (1.0 + helm[None, :] * jnp.repeat(mode_speed, 2)[:, None])
    out = pl.pallas_call(
        functools.partial(update_kernel, nb),
        grid=(pairs,),
        out_shape=jax.ShapeDtypeStruct((slots, nfld, 2, ndeg), F32),
        in_specs=[
            smem,
            smem,
            pl.BlockSpec((nb, JPAD, LANES), lambda j: (0, 0, 0)),
            pl.BlockSpec((2, nfld, 2, ndeg), lambda j: (j, 0, 0, 0)),
            pl.BlockSpec((2, nlat, ndeg), lambda j: (j, 0, 0)),
            pl.BlockSpec((2 * nfld, ndeg), lambda j: (0, 0)),
        ],
        out_specs=pl.BlockSpec((2, nfld, 2, ndeg), lambda j: (j, 0, 0, 0)),
        scratch_shapes=[
            pltpu.VMEM((nb, JPAD, LANES), F32),
            pltpu.VMEM((nlat, LANES), F32),
            pltpu.VMEM((8, LANES), F32),
        ],
    )(slot_wave, row_points, arrived, spec_rows, leg_rows, inverse)
    return out.transpose(0, 2, 1, 3)


def solution(mesh):
    return jax.shard_map(
        shards,
        mesh=mesh,
        in_specs=(P("band", None, "lev", None), P("band", None, None), P(), P(), P(), P(), P("lev")),
        out_specs=P("band", None, "lev", None),
        check_vma=False,
    )
```

```python
import functools

import jax
import jax.numpy as jnp
from jax import lax
from jax.experimental import pallas as pl
from jax.experimental.pallas import tpu as pltpu
from jax.sharding import PartitionSpec as P

TRUNC = 1279
FIELDS = 5
LEVELS = 24
FPAD = 16
LANES = 128
CHUNKS = 6
POINTS = CHUNKS * LANES
IMAGES = 8
JPAD = 8
F32 = jnp.float32
BF16 = jnp.bfloat16
I32 = jnp.int32
MESH = pl.DeviceIdType.MESH
NT = (((1,), (1,)), ((), ()))


def dot(a, b):
    return jnp.dot(a, b, preferred_element_type=F32)


def iota(shape, dim):
    return lax.broadcasted_iota(I32, shape, dim)


def lev_of_chunk(chunk):
    return chunk + chunk // 3


def quarter_turn_pair(quarters):
    nearest = jnp.round(quarters)
    u = quarters - nearest
    turn = nearest.astype(I32)
    u2 = u * u
    sin_u = u * (1.5707963 + u2 * (-0.6459640 + u2 * (0.07969087 + u2 * (-0.0046737664 + u2 * 0.00015148))))
    cos_u = 1.0 + u2 * (-1.2337005 + u2 * (0.25366950 + u2 * (-0.020863453 + u2 * 0.00091814)))
    odd = (turn & 1) == 1
    cos_v = jnp.where(odd, sin_u, cos_u)
    sin_v = jnp.where(odd, cos_u, sin_u)
    cos_v = jnp.where(((turn + 1) & 2) == 2, -cos_v, cos_v)
    sin_v = jnp.where((turn & 2) == 2, -sin_v, sin_v)
    return cos_v, sin_v


def base_points(p, first_points, second_points):
    first_count = first_points // 8 + 1
    second = p >= first_count
    index = jnp.where(second, p - first_count, p)
    length = jnp.where(second, second_points, first_points)
    return second, index, length, 8 * index <= length


def turn(wave, k):
    step = (jnp.maximum(wave, 0) * k) & 3
    real = jnp.where(step == 0, 1.0, jnp.where(step == 2, -1.0, 0.0))
    imag = jnp.where(step == 1, 1.0, jnp.where(step == 3, -1.0, 0.0))
    return real, imag


def round_kernel(
    nb,
    nl,
    wave_s,
    points_s,
    gauss_s,
    layer_s,
    spec_hbm,
    leg_hbm,
    out_ref,
    values_hbm,
    spec_ref,
    values_v,
    leg_v,
    wave_col,
    wave_row,
    mix,
    fsend32,
    fsend,
    frecv,
    cos_v,
    sin_v,
    coef,
    rep,
    cos_w,
    sin_w,
    gsend,
    grecv,
    terms32,
    tsend,
    trecv,
    sums,
    diffs,
    ztab,
    back,
    bsend,
    spec_sem,
    own_sem,
    values_sem,
    leg_sem,
    send_sem,
    recv_sem,
):
    slots = leg_v.shape[0]
    pairs = slots // 2
    ndeg = leg_v.shape[2]
    nfld = spec_ref.shape[1]
    half = nb * JPAD
    qblock = min(16, nb)
    rows = qblock * JPAD
    blocks = nb // qblock
    band = lax.axis_index("band")
    lev = lax.axis_index("lev")

    barrier = pltpu.get_barrier_semaphore()
    far = nb // 2

    def ahead(offset):
        return lax.rem(band + offset, nb)

    def each_peer(act):
        act(ahead(far))

        @pl.loop(1, far)
        def _(step):
            act(ahead(far - step))
            act(ahead(far + step))

    each_peer(lambda peer: pl.semaphore_signal(barrier, inc=1, device_id=(peer, lev), device_id_type=MESH))

    @pl.loop(1, nl)
    def _(step):
        pl.semaphore_signal(barrier, inc=1, device_id=(band, lax.rem(lev + step, nl)), device_id_type=MESH)

    spec_copy = pltpu.make_async_copy(spec_hbm, spec_ref, spec_sem)
    spec_copy.start()
    copies = [pltpu.make_async_copy(leg_hbm.at[s], leg_v.at[s], leg_sem.at[s]) for s in range(slots)]
    for copy in copies:
        copy.start()

    fsend32[...] = jnp.zeros_like(fsend32)
    degree = iota((FPAD, ndeg), 1)
    blank = jnp.zeros((4 * FPAD, ndeg), BF16)
    fill = jnp.zeros((FPAD - nfld, ndeg), F32)
    second_lane = (iota((nb, LANES), 1) // (2 * FPAD)) % 2 == 1
    spec_copy.wait()
    for j in range(pairs):
        parts = []
        for parity in range(2):
            s = 2 * j + parity
            wave = wave_s[band * slots + s]
            first_degree = jnp.where(wave < 0, ndeg, wave)
            loaded = spec_ref[s].astype(F32)
            components = []
            for component in range(2):
                values = jnp.concatenate([loaded[:, component, :], fill], axis=0)
                components.append(jnp.where(degree >= first_degree, values, 0.0).astype(BF16))
            values_v[s] = jnp.concatenate(components, axis=0)
            values = values_v[s]
            whole = [values, values, blank] if parity == 0 else [blank, values, values]
            copies[s].wait()
            parts.append(
                lax.dot_general(leg_v[s], jnp.concatenate(whole, axis=0), NT, preferred_element_type=F32)
            )
        mix[...] = parts[0] + parts[1]
        first = mix[pl.ds(0, nb, stride=2), :]
        other = mix[pl.ds(1, nb, stride=2), :]
        fsend32[:, j, :] = jnp.where(second_lane, other, first)

    values_copy = pltpu.make_async_copy(values_v, values_hbm, values_sem)
    values_copy.start()

    @pl.loop(0, blocks)
    def _(b):
        fsend[pl.ds(b * qblock, qblock)] = fsend32[pl.ds(b * qblock, qblock)].astype(BF16)

    pl.semaphore_wait(barrier, nb - 1 + nl - 1)

    def send_coefficients(peer):
        pltpu.make_async_remote_copy(
            src_ref=fsend.at[peer],
            dst_ref=frecv.at[band],
            send_sem=send_sem.at[0],
            recv_sem=recv_sem.at[0],
            device_id=(peer, lev),
            device_id_type=MESH,
        ).start()

    each_peer(send_coefficients)
    frecv[band] = fsend[band]

    first_points = points_s[2 * band]
    second_points = points_s[2 * band + 1]

    row8 = iota((JPAD, LANES), 0)

    @pl.loop(0, nb)
    def _(q):
        for parity in range(2):
            column = jnp.full((JPAD, LANES), -1, I32)
            for j in range(pairs):
                column = jnp.where(row8 == j, wave_s[q * slots + 2 * j + parity], column)
            wave_col[pl.ds(pl.multiple_of(parity * half + q * JPAD, JPAD), JPAD), :] = column

    lane_k = iota((rows, LANES), 1)
    flip = jnp.where((lane_k // 4) % 2 == 0, -1.0, 1.0)
    for b in range(2 * blocks):
        cut = pl.ds(b * rows, rows)
        column = wave_col[cut, :]
        real, imag = turn(column, lane_k % 4)
        mult = jnp.where(column < 0, 0.0, jnp.where(column == 0, 1.0, 2.0))
        coef[0, cut] = real * mult
        coef[1, cut] = -imag * mult
        coef[2, cut] = flip * real * mult
        coef[3, cut] = flip * imag * mult
        turned = column.astype(F32).T[:16]
        wave_row[:, cut] = turned
        row_re, row_im = turn(turned[:8].astype(I32), iota((8, rows), 0) % 4)
        ztab[:, cut] = jnp.where(iota((8, rows), 0) < 4, row_re, -row_im)

    @pl.loop(0, POINTS // 16)
    def _(i):
        p = i * 16 + iota((16, rows), 0)
        _, index, length, valid = base_points(p, first_points, second_points)
        length = length.astype(F32)
        inverse = 1.0 / length
        index = index.astype(F32)
        scale = 1.0 / jnp.sqrt(length)
        limit = jnp.where(valid, length - 1.0, -1.0)

        def angle(wave):
            product = wave * index
            residue = product - jnp.floor(product * inverse) * length
            return quarter_turn_pair(residue * (4.0 * inverse))

        whole_cos, whole_sin = angle(float(TRUNC))
        here = pl.ds(pl.multiple_of(i * 16, 16), 16)
        for lane in range(blocks):
            cut = pl.ds(lane * rows, rows)
            wave = wave_row[:, cut]
            cos_p, sin_p = angle(wave)
            height = jnp.where((2.0 * wave <= limit) & (wave >= 0.0), scale, 0.0)
            cos_v[here, cut] = (cos_p * height).astype(BF16)
            sin_v[here, cut] = (sin_p * height).astype(BF16)
            cut = pl.ds(half + lane * rows, rows)
            wave = wave_row[:, cut]
            height = jnp.where((2.0 * wave <= limit) & (wave >= 0.0), scale, 0.0)
            cos_v[here, cut] = ((whole_cos * cos_p + whole_sin * sin_p) * height).astype(BF16)
            sin_v[here, cut] = ((whole_sin * cos_p - whole_cos * sin_p) * height).astype(BF16)

    source = iota((LANES, 2 * LANES), 0)
    target = iota((LANES, 2 * LANES), 1)
    wanted = (target // LANES) * (2 * FPAD) + (target % LANES) // IMAGES
    for parity in range(2):
        for component in range(2):
            hit = source == wanted + parity * 4 * FPAD + component * FPAD
            rep[2 * parity + component] = jnp.where(hit, 1.0, 0.0).astype(BF16)

    pltpu.make_async_copy(frecv.at[pl.ds(0, nb - 1)], frecv.at[pl.ds(0, nb - 1)], recv_sem.at[0]).wait()

    @pl.loop(0, blocks)
    def _(b):
        block = frecv[pl.ds(b * qblock, qblock)].reshape(rows, LANES)
        for parity in range(2):
            cut = pl.ds(pl.multiple_of(parity * half + b * rows, rows), rows)
            part_re = dot(block, rep[2 * parity])
            part_im = dot(block, rep[2 * parity + 1])
            for row in range(2):
                lanes = slice(row * LANES, row * LANES + LANES)
                re, im = part_re[:, lanes], part_im[:, lanes]
                cos_w[cut, lanes] = (coef[0, cut] * re + coef[1, cut] * im).astype(BF16)
                sin_w[cut, lanes] = (coef[2, cut] * im + coef[3, cut] * re).astype(BF16)

    def send_points(chunk):
        target_lev = lev_of_chunk(chunk)

        @pl.when(lev != target_lev)
        def _():
            pltpu.make_async_remote_copy(
                src_ref=gsend.at[chunk, pl.ds(0, nfld)],
                dst_ref=grecv.at[lev, pl.ds(0, nfld)],
                send_sem=send_sem.at[1],
                recv_sem=recv_sem.at[1],
                device_id=(band, target_lev),
                device_id_type=MESH,
            ).start()

        @pl.when(lev == target_lev)
        def _():
            grecv[lev] = gsend[chunk]

    for c in range(CHUNKS // 2):
        cut = slice(c * 2 * LANES, (c + 1) * 2 * LANES)
        values = dot(cos_v[cut, :], cos_w[...]) + dot(sin_v[cut, :], sin_w[...])
        for part in range(2):
            here = slice(part * LANES, part * LANES + LANES)
            p = (2 * c + part) * LANES + iota((LANES, LANES), 0)
            second, _, _, _ = base_points(p, first_points, second_points)
            chosen = jnp.where(second, values[here, LANES:], values[here, :LANES])
            gsend[2 * c + part] = chosen.T.astype(BF16).reshape(FPAD, IMAGES, LANES)
            send_points(2 * c + part)

    works = lax.rem(lev, 4) != 3

    @pl.when(works)
    def _():
        others = grecv.at[pl.ds(0, nl - 1), pl.ds(0, nfld)]
        pltpu.make_async_copy(others, others, recv_sem.at[1]).wait()
        chunk = lev - lev // 4
        terms32[...] = jnp.zeros_like(terms32)

        def get(field, level):
            f = field * LEVELS + level
            return grecv[f // nfld, f % nfld].astype(F32)

        def put(field, level, value):
            f = field * LEVELS + level
            terms32[f // nfld, :, f % nfld, :] = value

        total = jnp.zeros((IMAGES, LANES), F32)
        for level in reversed(range(LEVELS)):
            wind_u, wind_v, temper = get(0, level), get(1, level), get(2, level)
            total = total + layer_s[level] * temper
            put(0, level, wind_u * temper)
            put(1, level, wind_v * temper)
            put(2, level, wind_u * get(3, level))
            put(3, level, wind_v * get(4, level))
            put(4, level, 0.5 * (wind_u * wind_u + wind_v * wind_v) + total)
        for target_lev in range(nl):
            tsend[target_lev] = terms32[target_lev].reshape(LANES, LANES).astype(BF16)

        @pl.loop(1, nl)
        def _(step):
            peer = lax.rem(lev + step, nl)
            pltpu.make_async_remote_copy(
                src_ref=tsend.at[peer],
                dst_ref=trecv.at[chunk],
                send_sem=send_sem.at[2],
                recv_sem=recv_sem.at[2],
                device_id=(band, peer),
                device_id_type=MESH,
            ).start()

        trecv[chunk] = tsend[lev]
        pltpu.make_async_copy(
            trecv.at[pl.ds(0, CHUNKS - 1)], trecv.at[pl.ds(0, CHUNKS - 1)], recv_sem.at[2]
        ).wait()

    @pl.when(jnp.logical_not(works))
    def _():
        pltpu.make_async_copy(trecv, trecv, recv_sem.at[2]).wait()

    for chunk in range(CHUNKS):
        p = chunk * LANES + iota((1, LANES), 1)
        second, index, length, valid = base_points(p, first_points, second_points)
        alone = (index == 0) | (8 * index == length)
        keep = jnp.where(valid, jnp.where(alone, 0.5, 1.0), 0.0)
        pieces = trecv[chunk].astype(F32)
        plus, minus = pieces[: 4 * FPAD], pieces[4 * FPAD :]
        lanes = slice(chunk * LANES, chunk * LANES + LANES)
        for row in range(2):
            kept = jnp.where(second, keep, 0.0) if row else jnp.where(second, 0.0, keep)
            to = slice(row * 4 * FPAD, (row + 1) * 4 * FPAD)
            sums[to, lanes] = ((plus + minus) * kept).astype(BF16)
            diffs[to, lanes] = ((plus - minus) * kept).astype(BF16)

    home = band // qblock
    order = sorted(range(blocks), key=lambda away: -min(away, blocks - away))
    for away in order:
        b = lax.rem(home + away, blocks)
        cuts = [pl.ds(pl.multiple_of(parity * half + b * rows, rows), rows) for parity in range(2)]

        def both(ref, at):
            return jnp.concatenate([ref[at, cut] for cut in cuts], axis=1)

        cos_z = dot(sums[...], both(cos_v, slice(None)))
        sin_z = dot(diffs[...], both(sin_v, slice(None)))
        for row in range(2):
            re = jnp.zeros((FPAD, 2 * rows), F32)
            im = jnp.zeros((FPAD, 2 * rows), F32)
            for k in range(4):
                at = (row * 4 + k) * FPAD
                zr, zi = both(ztab, pl.ds(k, 1)), both(ztab, pl.ds(4 + k, 1))
                cz, sz = cos_z[at : at + FPAD], sin_z[at : at + FPAD]
                re = re + zr * cz + zi * sz
                im = im + zi * cz - zr * sz
            weight = gauss_s[2 * band + row]
            for parity in range(2):
                at = parity * 4 * FPAD + row * 2 * FPAD
                lanes = slice(parity * rows, (parity + 1) * rows)
                back[pl.ds(at, FPAD), :] = re[:, lanes] * weight
                back[pl.ds(at + FPAD, FPAD), :] = im[:, lanes] * weight
        bsend[pl.ds(b * qblock, qblock)] = back[...].T.astype(BF16).reshape(qblock, JPAD, LANES)

        @pl.loop(0, qblock)
        def _(t):
            peer = b * qblock + t

            @pl.when(peer != band)
            def _():
                pltpu.make_async_remote_copy(
                    src_ref=bsend.at[peer],
                    dst_ref=out_ref.at[band],
                    send_sem=send_sem.at[3],
                    recv_sem=recv_sem.at[3],
                    device_id=(peer, lev),
                    device_id_type=MESH,
                ).start()

    own_copy = pltpu.make_async_copy(bsend.at[band], out_ref.at[band], own_sem)
    own_copy.start()
    own_copy.wait()
    values_copy.wait()
    pltpu.make_async_copy(out_ref.at[pl.ds(0, nb - 1)], out_ref.at[pl.ds(0, nb - 1)], recv_sem.at[3]).wait()

    pltpu.make_async_copy(fsend.at[pl.ds(0, nb - 1)], fsend.at[pl.ds(0, nb - 1)], send_sem.at[0]).wait()
    pltpu.make_async_copy(bsend.at[pl.ds(0, nb - 1)], bsend.at[pl.ds(0, nb - 1)], send_sem.at[3]).wait()

    @pl.when(works)
    def _():
        others = gsend.at[pl.ds(0, CHUNKS - 1), pl.ds(0, nfld)]
        pltpu.make_async_copy(others, others, send_sem.at[1]).wait()
        pltpu.make_async_copy(tsend.at[pl.ds(0, nl - 1)], tsend.at[pl.ds(0, nl - 1)], send_sem.at[2]).wait()

    @pl.when(jnp.logical_not(works))
    def _():
        others = gsend.at[:, pl.ds(0, nfld)]
        pltpu.make_async_copy(others, others, send_sem.at[1]).wait()


def update_kernel(
    nb, wave_s, speed_s, arrived_hbm, values_hbm, leg_hbm, out_hbm, arrived, values_v, leg_v, out_v, inverse, wide, mix, turned, sems, leg_sem, out_sem
):
    band = lax.axis_index("band")
    slots, nlat, ndeg = leg_v.shape
    nfld = speed_s.shape[0]
    pairs = slots // 2
    cuts = 5
    width = ndeg // cuts
    lanes = min(LANES, width)
    tiles = width // lanes
    per_field = 2 * cuts * tiles
    waves = [wave_s[band * slots + s] for s in range(slots)]
    firsts = [jnp.where(wave < 0, ndeg, wave) for wave in waves]

    def piece(j, t):
        start = jnp.maximum(waves[2 * j], 0) // width
        later = t >= cuts - start
        return jnp.where(later, 1, 0), jnp.where(later, t - 1, start + t)

    def leg_copy(j, t):
        parity, block = piece(j, t)
        cut = pl.ds(pl.multiple_of(block * width, width), width)
        slot = 2 * j + parity
        return pltpu.make_async_copy(leg_hbm.at[slot, :, cut], leg_v.at[slot, :, cut], leg_sem.at[j])

    def values_copy(j):
        cut = pl.ds(2 * j, 2)
        return pltpu.make_async_copy(values_hbm.at[cut], values_v.at[cut], sems.at[1 + j])

    arrived_copy = pltpu.make_async_copy(arrived_hbm, arrived, sems.at[0])
    arrived_copy.start()
    for j in range(pairs):
        values_copy(j).start()
        for t in range(cuts + 1):
            leg_copy(j, t).start()

    field = iota((FPAD, lanes), 0)
    speed = jnp.zeros((FPAD, lanes), F32)
    for f in range(nfld):
        speed = jnp.where(field == f, speed_s[f], speed)
    for at in range(0, ndeg, lanes):
        n = at + iota((FPAD, lanes), 1)
        helm = (n * (n + 1)).astype(F32) / float(TRUNC * (TRUNC + 1))
        inverse[:, at : at + lanes] = 1.0 / (1.0 + helm * speed)
    out_v[...] = jnp.zeros_like(out_v)
    fits = (iota((nlat, LANES), 0) % 2) == (iota((nlat, LANES), 1) // (2 * FPAD)) % 2
    degree = iota((FPAD, width), 1)
    arrived_copy.wait()
    wide[...] = arrived[...].astype(F32)
    for j in range(pairs):
        mine = wide[:, j, :]
        mix[pl.ds(0, nb, stride=2), :] = mine
        mix[pl.ds(1, nb, stride=2), :] = mine
        flat = jnp.where(fits, mix[...], 0.0).T
        for parity in range(2):
            at = parity * 4 * FPAD
            turned[2 * j + parity] = (flat[at : at + 2 * FPAD] + flat[at + 2 * FPAD : at + 4 * FPAD]).astype(BF16)

    for j in range(pairs):
        values_copy(j).wait()
        for t in range(cuts + 1):
            leg_copy(j, t).wait()
        for t in range(cuts + 1):
            parity, block = piece(j, t)
            slot = 2 * j + parity
            first_degree = jnp.where(parity == 0, firsts[2 * j], firsts[2 * j + 1])
            cut = pl.ds(pl.multiple_of(block * width, width), width)
            tendency = dot(turned[slot], leg_v[slot, :, cut])
            sum_here = values_v[slot, :, cut].astype(F32) + tendency
            live = degree + block * width >= first_degree
            for component in range(2):
                part = sum_here[component * FPAD : (component + 1) * FPAD] * inverse[:, cut]
                part = jnp.where(live, part, 0.0)
                for tile in range(tiles):
                    row = slot * nfld * per_field + (block * tiles + tile) * 2 + component
                    out_v[pl.ds(row, nfld, stride=per_field), :] = part[:nfld, tile * lanes : (tile + 1) * lanes]
        here = pl.ds(2 * j * nfld * per_field, 2 * nfld * per_field)
        pltpu.make_async_copy(out_v.at[here], out_hbm.at[here], out_sem.at[j]).start()
    for j in range(pairs):
        here = pl.ds(2 * j * nfld * per_field, 2 * nfld * per_field)
        pltpu.make_async_copy(out_v.at[here], out_hbm.at[here], out_sem.at[j]).wait()


def shards(spectra, legendre, slot_wave, row_points, gauss_weight, layer_depth, mode_speed):
    slots, _, nfld, ndeg = spectra.shape
    nb = lax.axis_size("band")
    nl = lax.axis_size("lev")
    nlat = legendre.shape[2]
    pairs = slots // 2
    half = nb * JPAD
    rows = min(16, nb) * JPAD
    spec_rows = spectra.transpose(0, 2, 1, 3)
    leg_rows = legendre.transpose(0, 2, 1)
    smem = pl.BlockSpec(memory_space=pltpu.SMEM)
    anywhere = pl.BlockSpec(memory_space=pl.ANY)
    arrived, values = pl.pallas_call(
        functools.partial(round_kernel, nb, nl),
        out_shape=(
            jax.ShapeDtypeStruct((nb, JPAD, LANES), BF16),
            jax.ShapeDtypeStruct((slots, 2 * FPAD, ndeg), BF16),
        ),
        in_specs=[smem] * 4 + [anywhere, anywhere],
        out_specs=(anywhere, anywhere),
        scratch_shapes=[
            pltpu.VMEM((slots, nfld, 2, ndeg), BF16),
            pltpu.VMEM((slots, 2 * FPAD, ndeg), BF16),
            pltpu.VMEM((slots, nlat, ndeg), BF16),
            pltpu.VMEM((2 * half, LANES), I32),
            pltpu.VMEM((16, 2 * half), F32),
            pltpu.VMEM((nlat, LANES), F32),
            pltpu.VMEM((nb, JPAD, LANES), F32),
            pltpu.VMEM((nb, JPAD, LANES), BF16),
            pltpu.VMEM((nb, JPAD, LANES), BF16),
            pltpu.VMEM((POINTS, 2 * half), BF16),
            pltpu.VMEM((POINTS, 2 * half), BF16),
            pltpu.VMEM((4, 2 * half, LANES), F32),
            pltpu.VMEM((4, LANES, 2 * LANES), BF16),
            pltpu.VMEM((2 * half, 2 * LANES), BF16),
            pltpu.VMEM((2 * half, 2 * LANES), BF16),
            pltpu.VMEM((CHUNKS, FPAD, IMAGES, LANES), BF16),
            pltpu.VMEM((nl, FPAD, IMAGES, LANES), BF16),
            pltpu.VMEM((nl, IMAGES, FPAD, LANES), F32),
            pltpu.VMEM((nl, LANES, LANES), BF16),
            pltpu.VMEM((CHUNKS, LANES, LANES), BF16),
            pltpu.VMEM((LANES, POINTS), BF16),
            pltpu.VMEM((LANES, POINTS), BF16),
            pltpu.VMEM((8, 2 * half), F32),
            pltpu.VMEM((LANES, rows), F32),
            pltpu.VMEM((nb, JPAD, LANES), BF16),
            pltpu.SemaphoreType.DMA,
            pltpu.SemaphoreType.DMA,
            pltpu.SemaphoreType.DMA,
            pltpu.SemaphoreType.DMA((slots,)),
            pltpu.SemaphoreType.DMA((4,)),
            pltpu.SemaphoreType.DMA((4,)),
        ],
        compiler_params=pltpu.CompilerParams(
            collective_id=0, has_side_effects=True, vmem_limit_bytes=56 * 1024 * 1024
        ),
    )(slot_wave, row_points, gauss_weight, layer_depth, spec_rows, leg_rows)

    lanes = min(LANES, ndeg // 5)
    tiles = ndeg // lanes
    out = pl.pallas_call(
        functools.partial(update_kernel, nb),
        out_shape=jax.ShapeDtypeStruct((slots * nfld * tiles * 2, lanes), F32),
        in_specs=[smem, smem, anywhere, anywhere, anywhere],
        out_specs=anywhere,
        scratch_shapes=[
            pltpu.VMEM((nb, JPAD, LANES), BF16),
            pltpu.VMEM((slots, 2 * FPAD, ndeg), BF16),
            pltpu.VMEM((slots, nlat, ndeg), BF16),
            pltpu.VMEM((slots * nfld * tiles * 2, lanes), F32),
            pltpu.VMEM((FPAD, ndeg), F32),
            pltpu.VMEM((nb, JPAD, LANES), F32),
            pltpu.VMEM((nlat, LANES), F32),
            pltpu.VMEM((slots, 2 * FPAD, nlat), BF16),
            pltpu.SemaphoreType.DMA((1 + pairs,)),
            pltpu.SemaphoreType.DMA((pairs,)),
            pltpu.SemaphoreType.DMA((pairs,)),
        ],
        compiler_params=pltpu.CompilerParams(vmem_limit_bytes=56 * 1024 * 1024),
    )(slot_wave, mode_speed, arrived, values, leg_rows)
    out = out.reshape(slots, nfld, tiles, 2, lanes).transpose(0, 1, 3, 2, 4)
    return out.reshape(slots, nfld, 2, ndeg).transpose(0, 2, 1, 3)


def solution(mesh):
    return jax.shard_map(
        shards,
        mesh=mesh,
        in_specs=(P("band", None, "lev", None), P("band", None, None), P(), P(), P(), P(), P("lev")),
        out_specs=P("band", None, "lev", None),
        check_vma=False,
    )
```

```python
import functools

import jax
import jax.numpy as jnp
from jax import lax
from jax.experimental import pallas as pl
from jax.experimental.pallas import tpu as pltpu
from jax.sharding import PartitionSpec as P

TRUNC = 1279
FIELDS = 5
LEVELS = 24
FPAD = 16
LANES = 128
CHUNKS = 6
POINTS = CHUNKS * LANES
IMAGES = 8
JPAD = 8
F32 = jnp.float32
BF16 = jnp.bfloat16
I32 = jnp.int32
MESH = pl.DeviceIdType.MESH
NT = (((1,), (1,)), ((), ()))


def dot(a, b):
    return jnp.dot(a, b, preferred_element_type=F32)


def iota(shape, dim):
    return lax.broadcasted_iota(I32, shape, dim)


def lev_of_chunk(chunk):
    return chunk + chunk // 3


def half_turn_pair(u):
    u2 = u * u
    sin_u = u * (3.14158202 + u2 * (-5.16714279 + u2 * (2.54189895 + u2 * -0.554635995)))
    cos_u = 1.0 + u2 * (-4.93479552 + u2 * (4.05845134 + u2 * (-1.33209382 + u2 * 0.220080563)))
    return cos_u, sin_u


def base_points(p, first_points, second_points):
    first_count = first_points // 8 + 1
    second = p >= first_count
    index = jnp.where(second, p - first_count, p)
    length = jnp.where(second, second_points, first_points)
    return second, index, length, 8 * index <= length


def turn(wave, k):
    step = (jnp.maximum(wave, 0) * k) & 3
    real = jnp.where(step == 0, 1.0, jnp.where(step == 2, -1.0, 0.0))
    imag = jnp.where(step == 1, 1.0, jnp.where(step == 3, -1.0, 0.0))
    return real, imag


def round_kernel(
    nb,
    nl,
    wave_s,
    points_s,
    gauss_s,
    layer_s,
    spec_hbm,
    leg_hbm,
    out_ref,
    values_hbm,
    spec_ref,
    values_v,
    leg_v,
    wave_col,
    wave_row,
    mix,
    fsend32,
    fsend,
    frecv,
    cos_v,
    sin_v,
    coef,
    rep,
    cos_w,
    sin_w,
    gsend,
    grecv,
    terms32,
    tsend,
    trecv,
    sums,
    diffs,
    ztab,
    back,
    bsend,
    spec_sem,
    own_sem,
    values_sem,
    leg_sem,
    send_sem,
    recv_sem,
):
    slots = leg_v.shape[0]
    pairs = slots // 2
    ndeg = leg_v.shape[2]
    nfld = spec_ref.shape[1]
    half = nb * JPAD
    qblock = min(16, nb)
    rows = qblock * JPAD
    blocks = nb // qblock
    band = lax.axis_index("band")
    lev = lax.axis_index("lev")

    barrier = pltpu.get_barrier_semaphore()
    far = nb // 2

    def ahead(offset):
        return lax.rem(band + offset, nb)

    def each_peer(act):
        act(ahead(far))

        @pl.loop(1, far)
        def _(step):
            act(ahead(far - step))
            act(ahead(far + step))

    each_peer(lambda peer: pl.semaphore_signal(barrier, inc=1, device_id=(peer, lev), device_id_type=MESH))

    @pl.loop(1, nl)
    def _(step):
        pl.semaphore_signal(barrier, inc=1, device_id=(band, lax.rem(lev + step, nl)), device_id_type=MESH)

    spec_copy = pltpu.make_async_copy(spec_hbm, spec_ref, spec_sem)
    spec_copy.start()
    copies = [pltpu.make_async_copy(leg_hbm.at[s], leg_v.at[s], leg_sem.at[s]) for s in range(slots)]
    for copy in copies:
        copy.start()

    fsend32[...] = jnp.zeros_like(fsend32)
    degree = iota((2 * FPAD, ndeg), 1)
    blank = jnp.zeros((4 * FPAD, ndeg), BF16)
    fill = jnp.zeros((2 * FPAD - 2 * nfld, ndeg), BF16)
    second_lane = (iota((nb, LANES), 1) // (2 * FPAD)) % 2 == 1
    spec_copy.wait()
    for j in range(pairs):
        parts = []
        for parity in range(2):
            s = 2 * j + parity
            wave = wave_s[band * slots + s]
            values = spec_ref[s].reshape(2 * nfld, ndeg)
            values = jnp.concatenate([values, fill], axis=0)
            first_degree = jnp.where(wave < 0, ndeg, wave)
            values = jnp.where(degree >= first_degree, values.astype(F32), 0.0).astype(BF16)
            whole = [values, values, blank] if parity == 0 else [blank, values, values]
            copies[s].wait()
            parts.append(
                lax.dot_general(leg_v[s], jnp.concatenate(whole, axis=0), NT, preferred_element_type=F32)
            )
        mix[...] = parts[0] + parts[1]
        first = mix[pl.ds(0, nb, stride=2), :]
        other = mix[pl.ds(1, nb, stride=2), :]
        fsend32[:, j, :] = jnp.where(second_lane, other, first)

    @pl.loop(0, blocks)
    def _(b):
        fsend[pl.ds(b * qblock, qblock)] = fsend32[pl.ds(b * qblock, qblock)].astype(BF16)

    pl.semaphore_wait(barrier, nb - 1 + nl - 1)

    def send_coefficients(peer):
        pltpu.make_async_remote_copy(
            src_ref=fsend.at[peer],
            dst_ref=frecv.at[band],
            send_sem=send_sem.at[0],
            recv_sem=recv_sem.at[0],
            device_id=(peer, lev),
            device_id_type=MESH,
        ).start()

    each_peer(send_coefficients)
    frecv[band] = fsend[band]

    first_points = points_s[2 * band]
    second_points = points_s[2 * band + 1]

    row8 = iota((JPAD, LANES), 0)

    @pl.loop(0, nb)
    def _(q):
        for parity in range(2):
            column = jnp.full((JPAD, LANES), -1, I32)
            for j in range(pairs):
                column = jnp.where(row8 == j, wave_s[q * slots + 2 * j + parity], column)
            wave_col[pl.ds(pl.multiple_of(parity * half + q * JPAD, JPAD), JPAD), :] = column

    lane_k = iota((rows, LANES), 1)
    flip = jnp.where((lane_k // 4) % 2 == 0, -1.0, 1.0)
    for b in range(2 * blocks):
        cut = pl.ds(b * rows, rows)
        column = wave_col[cut, :]
        real, imag = turn(column, lane_k % 4)
        mult = jnp.where(column < 0, 0.0, jnp.where(column == 0, 1.0, 2.0))
        coef[0, cut] = real * mult
        coef[1, cut] = -imag * mult
        coef[2, cut] = flip * real * mult
        coef[3, cut] = flip * imag * mult
        turned = column.astype(F32).T[:16]
        wave_row[:, cut] = jnp.where(turned < 0.0, 1.0e5, turned)
        row_re, row_im = turn(turned[:8].astype(I32), iota((8, rows), 0) % 4)
        ztab[:, cut] = jnp.where(iota((8, rows), 0) < 4, row_re, -row_im)

    @pl.loop(0, POINTS // 16)
    def _(i):
        p = i * 16 + iota((16, rows), 0)
        _, index, length, valid = base_points(p, first_points, second_points)
        length = length.astype(F32)
        inverse = 1.0 / length
        doubled = 2.0 * index.astype(F32)
        scale = 1.0 / jnp.sqrt(length)
        limit = jnp.where(valid, 0.5 * (length - 1.0), -1.0)

        def angle(wave):
            product = wave * doubled
            nearest = jnp.round(product * inverse)
            cos_u, sin_u = half_turn_pair((product - nearest * length) * inverse)
            return cos_u, sin_u, (nearest.astype(I32) & 1) == 1

        whole_cos, whole_sin, odd = angle(float(TRUNC))
        whole_cos = jnp.where(odd, -whole_cos, whole_cos)
        whole_sin = jnp.where(odd, -whole_sin, whole_sin)
        here = pl.ds(pl.multiple_of(i * 16, 16), 16)
        for lane in range(blocks):
            cut = pl.ds(lane * rows, rows)
            wave = wave_row[:, cut]
            cos_p, sin_p, odd = angle(wave)
            signed = jnp.where(odd, -scale, scale)
            height = jnp.where(wave <= limit, signed, 0.0)
            cos_v[here, cut] = (cos_p * height).astype(BF16)
            sin_v[here, cut] = (sin_p * height).astype(BF16)
            cut = pl.ds(half + lane * rows, rows)
            height = jnp.where(wave_row[:, cut] <= limit, signed, 0.0)
            cos_v[here, cut] = ((whole_cos * cos_p + whole_sin * sin_p) * height).astype(BF16)
            sin_v[here, cut] = ((whole_sin * cos_p - whole_cos * sin_p) * height).astype(BF16)

    source = iota((LANES, 2 * LANES), 0)
    target = iota((LANES, 2 * LANES), 1)
    wanted = (target // LANES) * (2 * FPAD) + (target % LANES) // IMAGES * 2
    for parity in range(2):
        for component in range(2):
            hit = source == wanted + parity * 4 * FPAD + component
            rep[2 * parity + component] = jnp.where(hit, 1.0, 0.0).astype(BF16)

    pltpu.make_async_copy(frecv.at[pl.ds(0, nb - 1)], frecv.at[pl.ds(0, nb - 1)], recv_sem.at[0]).wait()

    @pl.loop(0, blocks)
    def _(b):
        block = frecv[pl.ds(b * qblock, qblock)].reshape(rows, LANES)
        for parity in range(2):
            cut = pl.ds(pl.multiple_of(parity * half + b * rows, rows), rows)
            part_re = dot(block, rep[2 * parity])
            part_im = dot(block, rep[2 * parity + 1])
            for row in range(2):
                lanes = slice(row * LANES, row * LANES + LANES)
                re, im = part_re[:, lanes], part_im[:, lanes]
                cos_w[cut, lanes] = (coef[0, cut] * re + coef[1, cut] * im).astype(BF16)
                sin_w[cut, lanes] = (coef[2, cut] * im + coef[3, cut] * re).astype(BF16)

    def send_points(chunk):
        target_lev = lev_of_chunk(chunk)

        @pl.when(lev != target_lev)
        def _():
            pltpu.make_async_remote_copy(
                src_ref=gsend.at[chunk, pl.ds(0, nfld)],
                dst_ref=grecv.at[lev, pl.ds(0, nfld)],
                send_sem=send_sem.at[1],
                recv_sem=recv_sem.at[1],
                device_id=(band, target_lev),
                device_id_type=MESH,
            ).start()

        @pl.when(lev == target_lev)
        def _():
            grecv[lev] = gsend[chunk]

    for c in range(CHUNKS // 2):
        cut = slice(c * 2 * LANES, (c + 1) * 2 * LANES)
        values = dot(cos_v[cut, :], cos_w[...]) + dot(sin_v[cut, :], sin_w[...])
        for part in range(2):
            here = slice(part * LANES, part * LANES + LANES)
            p = (2 * c + part) * LANES + iota((LANES, LANES), 0)
            second, _, _, _ = base_points(p, first_points, second_points)
            chosen = jnp.where(second, values[here, LANES:], values[here, :LANES])
            gsend[2 * c + part] = chosen.T.astype(BF16).reshape(FPAD, IMAGES, LANES)
            send_points(2 * c + part)

    works = lax.rem(lev, 4) != 3

    @pl.when(works)
    def _():
        others = grecv.at[pl.ds(0, nl - 1), pl.ds(0, nfld)]
        pltpu.make_async_copy(others, others, recv_sem.at[1]).wait()
        chunk = lev - lev // 4
        terms32[...] = jnp.zeros_like(terms32)

        def get(field, level):
            f = field * LEVELS + level
            return grecv[f // nfld, f % nfld].astype(F32)

        def put(field, level, value):
            f = field * LEVELS + level
            terms32[f // nfld, :, f % nfld, :] = value

        total = jnp.zeros((IMAGES, LANES), F32)
        for level in reversed(range(LEVELS)):
            wind_u, wind_v, temper = get(0, level), get(1, level), get(2, level)
            total = total + layer_s[level] * temper
            put(0, level, wind_u * temper)
            put(1, level, wind_v * temper)
            put(2, level, wind_u * get(3, level))
            put(3, level, wind_v * get(4, level))
            put(4, level, 0.5 * (wind_u * wind_u + wind_v * wind_v) + total)
        for target_lev in range(nl):
            tsend[target_lev] = terms32[target_lev].reshape(LANES, LANES).astype(BF16)

        @pl.loop(1, nl)
        def _(step):
            peer = lax.rem(lev + step, nl)
            pltpu.make_async_remote_copy(
                src_ref=tsend.at[peer],
                dst_ref=trecv.at[chunk],
                send_sem=send_sem.at[2],
                recv_sem=recv_sem.at[2],
                device_id=(band, peer),
                device_id_type=MESH,
            ).start()

        trecv[chunk] = tsend[lev]
        pltpu.make_async_copy(
            trecv.at[pl.ds(0, CHUNKS - 1)], trecv.at[pl.ds(0, CHUNKS - 1)], recv_sem.at[2]
        ).wait()

    @pl.when(jnp.logical_not(works))
    def _():
        pltpu.make_async_copy(trecv, trecv, recv_sem.at[2]).wait()

    for chunk in range(CHUNKS):
        p = chunk * LANES + iota((1, LANES), 1)
        second, index, length, valid = base_points(p, first_points, second_points)
        alone = (index == 0) | (8 * index == length)
        keep = jnp.where(valid, jnp.where(alone, 0.5, 1.0), 0.0)
        pieces = trecv[chunk].astype(F32)
        plus, minus = pieces[: 4 * FPAD], pieces[4 * FPAD :]
        lanes = slice(chunk * LANES, chunk * LANES + LANES)
        for row in range(2):
            kept = jnp.where(second, keep, 0.0) if row else jnp.where(second, 0.0, keep)
            to = slice(row * 4 * FPAD, (row + 1) * 4 * FPAD)
            sums[to, lanes] = ((plus + minus) * kept).astype(BF16)
            diffs[to, lanes] = ((plus - minus) * kept).astype(BF16)

    home = band // qblock
    order = sorted(range(blocks), key=lambda away: -min(away, blocks - away))
    for away in order:
        b = lax.rem(home + away, blocks)
        cuts = [pl.ds(pl.multiple_of(parity * half + b * rows, rows), rows) for parity in range(2)]

        def both(ref, at):
            return jnp.concatenate([ref[at, cut] for cut in cuts], axis=1)

        cos_z = dot(sums[...], both(cos_v, slice(None)))
        sin_z = dot(diffs[...], both(sin_v, slice(None)))
        for row in range(2):
            re = jnp.zeros((FPAD, 2 * rows), F32)
            im = jnp.zeros((FPAD, 2 * rows), F32)
            for k in range(4):
                at = (row * 4 + k) * FPAD
                zr, zi = both(ztab, pl.ds(k, 1)), both(ztab, pl.ds(4 + k, 1))
                cz, sz = cos_z[at : at + FPAD], sin_z[at : at + FPAD]
                re = re + zr * cz + zi * sz
                im = im + zi * cz - zr * sz
            weight = gauss_s[2 * band + row]
            for parity in range(2):
                at = parity * 4 * FPAD + row * 2 * FPAD
                lanes = slice(parity * rows, (parity + 1) * rows)
                back[pl.ds(at, FPAD), :] = re[:, lanes] * weight
                back[pl.ds(at + FPAD, FPAD), :] = im[:, lanes] * weight
        bsend[pl.ds(b * qblock, qblock)] = back[...].T.astype(BF16).reshape(qblock, JPAD, LANES)

        @pl.loop(0, qblock)
        def _(t):
            peer = b * qblock + t

            @pl.when(peer != band)
            def _():
                pltpu.make_async_remote_copy(
                    src_ref=bsend.at[peer],
                    dst_ref=out_ref.at[band],
                    send_sem=send_sem.at[3],
                    recv_sem=recv_sem.at[3],
                    device_id=(peer, lev),
                    device_id_type=MESH,
                ).start()

    own_copy = pltpu.make_async_copy(bsend.at[band], out_ref.at[band], own_sem)
    own_copy.start()

    fill = jnp.zeros((FPAD - nfld, ndeg), F32)
    for s in range(slots):
        loaded = spec_ref[s].astype(F32)
        components = [jnp.concatenate([loaded[:, c, :], fill], axis=0).astype(BF16) for c in range(2)]
        values_v[s] = jnp.concatenate(components, axis=0)
    values_copy = pltpu.make_async_copy(values_v, values_hbm, values_sem)
    values_copy.start()
    own_copy.wait()
    values_copy.wait()
    pltpu.make_async_copy(out_ref.at[pl.ds(0, nb - 1)], out_ref.at[pl.ds(0, nb - 1)], recv_sem.at[3]).wait()

    pltpu.make_async_copy(fsend.at[pl.ds(0, nb - 1)], fsend.at[pl.ds(0, nb - 1)], send_sem.at[0]).wait()
    pltpu.make_async_copy(bsend.at[pl.ds(0, nb - 1)], bsend.at[pl.ds(0, nb - 1)], send_sem.at[3]).wait()

    @pl.when(works)
    def _():
        others = gsend.at[pl.ds(0, CHUNKS - 1), pl.ds(0, nfld)]
        pltpu.make_async_copy(others, others, send_sem.at[1]).wait()
        pltpu.make_async_copy(tsend.at[pl.ds(0, nl - 1)], tsend.at[pl.ds(0, nl - 1)], send_sem.at[2]).wait()

    @pl.when(jnp.logical_not(works))
    def _():
        others = gsend.at[:, pl.ds(0, nfld)]
        pltpu.make_async_copy(others, others, send_sem.at[1]).wait()


def update_kernel(
    nb, wave_s, speed_s, arrived_hbm, values_hbm, leg_hbm, out_hbm, arrived, values_v, leg_v, out_v, inverse, wide, mix, turned, sems, leg_sem, out_sem
):
    band = lax.axis_index("band")
    slots, nlat, ndeg = leg_v.shape
    nfld = speed_s.shape[0]
    pairs = slots // 2
    cuts = 5
    width = ndeg // cuts
    lanes = min(LANES, width)
    tiles = width // lanes
    per_field = 2 * cuts * tiles
    waves = [wave_s[band * slots + s] for s in range(slots)]
    firsts = [jnp.where(wave < 0, ndeg, wave) for wave in waves]

    def piece(j, t):
        start = jnp.maximum(waves[2 * j], 0) // width
        later = t >= cuts - start
        return jnp.where(later, 1, 0), jnp.where(later, t - 1, start + t)

    def leg_copy(j, t):
        parity, block = piece(j, t)
        cut = pl.ds(pl.multiple_of(block * width, width), width)
        slot = 2 * j + parity
        return pltpu.make_async_copy(leg_hbm.at[slot, :, cut], leg_v.at[slot, :, cut], leg_sem.at[j])

    def values_copy(j):
        cut = pl.ds(2 * j, 2)
        return pltpu.make_async_copy(values_hbm.at[cut], values_v.at[cut], sems.at[1 + j])

    arrived_copy = pltpu.make_async_copy(arrived_hbm, arrived, sems.at[0])
    arrived_copy.start()
    for j in range(pairs):
        values_copy(j).start()
        for t in range(cuts + 1):
            leg_copy(j, t).start()

    field = iota((FPAD, lanes), 0)
    speed = jnp.zeros((FPAD, lanes), F32)
    for f in range(nfld):
        speed = jnp.where(field == f, speed_s[f], speed)
    for at in range(0, ndeg, lanes):
        n = at + iota((FPAD, lanes), 1)
        helm = (n * (n + 1)).astype(F32) / float(TRUNC * (TRUNC + 1))
        inverse[:, at : at + lanes] = 1.0 / (1.0 + helm * speed)
    out_v[...] = jnp.zeros_like(out_v)
    fits = (iota((nlat, LANES), 0) % 2) == (iota((nlat, LANES), 1) // (2 * FPAD)) % 2
    degree = iota((FPAD, width), 1)
    arrived_copy.wait()
    wide[...] = arrived[...].astype(F32)
    for j in range(pairs):
        mine = wide[:, j, :]
        mix[pl.ds(0, nb, stride=2), :] = mine
        mix[pl.ds(1, nb, stride=2), :] = mine
        flat = jnp.where(fits, mix[...], 0.0).T
        for parity in range(2):
            at = parity * 4 * FPAD
            turned[2 * j + parity] = (flat[at : at + 2 * FPAD] + flat[at + 2 * FPAD : at + 4 * FPAD]).astype(BF16)

    for j in range(pairs):
        values_copy(j).wait()
        for t in range(cuts + 1):
            leg_copy(j, t).wait()
        for t in range(cuts + 1):
            parity, block = piece(j, t)
            slot = 2 * j + parity
            first_degree = jnp.where(parity == 0, firsts[2 * j], firsts[2 * j + 1])
            cut = pl.ds(pl.multiple_of(block * width, width), width)
            tendency = dot(turned[slot], leg_v[slot, :, cut])
            sum_here = values_v[slot, :, cut].astype(F32) + tendency
            live = degree + block * width >= first_degree
            for component in range(2):
                part = sum_here[component * FPAD : (component + 1) * FPAD] * inverse[:, cut]
                part = jnp.where(live, part, 0.0)
                for tile in range(tiles):
                    row = slot * nfld * per_field + (block * tiles + tile) * 2 + component
                    out_v[pl.ds(row, nfld, stride=per_field), :] = part[:nfld, tile * lanes : (tile + 1) * lanes]
        here = pl.ds(2 * j * nfld * per_field, 2 * nfld * per_field)
        pltpu.make_async_copy(out_v.at[here], out_hbm.at[here], out_sem.at[j]).start()
    for j in range(pairs):
        here = pl.ds(2 * j * nfld * per_field, 2 * nfld * per_field)
        pltpu.make_async_copy(out_v.at[here], out_hbm.at[here], out_sem.at[j]).wait()


def shards(spectra, legendre, slot_wave, row_points, gauss_weight, layer_depth, mode_speed):
    slots, _, nfld, ndeg = spectra.shape
    nb = lax.axis_size("band")
    nl = lax.axis_size("lev")
    nlat = legendre.shape[2]
    pairs = slots // 2
    half = nb * JPAD
    rows = min(16, nb) * JPAD
    spec_rows = spectra.transpose(0, 2, 1, 3)
    leg_rows = legendre.transpose(0, 2, 1)
    smem = pl.BlockSpec(memory_space=pltpu.SMEM)
    anywhere = pl.BlockSpec(memory_space=pl.ANY)
    arrived, values = pl.pallas_call(
        functools.partial(round_kernel, nb, nl),
        out_shape=(
            jax.ShapeDtypeStruct((nb, JPAD, LANES), BF16),
            jax.ShapeDtypeStruct((slots, 2 * FPAD, ndeg), BF16),
        ),
        in_specs=[smem] * 4 + [anywhere, anywhere],
        out_specs=(anywhere, anywhere),
        scratch_shapes=[
            pltpu.VMEM((slots, nfld, 2, ndeg), BF16),
            pltpu.VMEM((slots, 2 * FPAD, ndeg), BF16),
            pltpu.VMEM((slots, nlat, ndeg), BF16),
            pltpu.VMEM((2 * half, LANES), I32),
            pltpu.VMEM((16, 2 * half), F32),
            pltpu.VMEM((nlat, LANES), F32),
            pltpu.VMEM((nb, JPAD, LANES), F32),
            pltpu.VMEM((nb, JPAD, LANES), BF16),
            pltpu.VMEM((nb, JPAD, LANES), BF16),
            pltpu.VMEM((POINTS, 2 * half), BF16),
            pltpu.VMEM((POINTS, 2 * half), BF16),
            pltpu.VMEM((4, 2 * half, LANES), F32),
            pltpu.VMEM((4, LANES, 2 * LANES), BF16),
            pltpu.VMEM((2 * half, 2 * LANES), BF16),
            pltpu.VMEM((2 * half, 2 * LANES), BF16),
            pltpu.VMEM((CHUNKS, FPAD, IMAGES, LANES), BF16),
            pltpu.VMEM((nl, FPAD, IMAGES, LANES), BF16),
            pltpu.VMEM((nl, IMAGES, FPAD, LANES), F32),
            pltpu.VMEM((nl, LANES, LANES), BF16),
            pltpu.VMEM((CHUNKS, LANES, LANES), BF16),
            pltpu.VMEM((LANES, POINTS), BF16),
            pltpu.VMEM((LANES, POINTS), BF16),
            pltpu.VMEM((8, 2 * half), F32),
            pltpu.VMEM((LANES, rows), F32),
            pltpu.VMEM((nb, JPAD, LANES), BF16),
            pltpu.SemaphoreType.DMA,
            pltpu.SemaphoreType.DMA,
            pltpu.SemaphoreType.DMA,
            pltpu.SemaphoreType.DMA((slots,)),
            pltpu.SemaphoreType.DMA((4,)),
            pltpu.SemaphoreType.DMA((4,)),
        ],
        compiler_params=pltpu.CompilerParams(
            collective_id=0, has_side_effects=True, vmem_limit_bytes=56 * 1024 * 1024
        ),
    )(slot_wave, row_points, gauss_weight, layer_depth, spec_rows, leg_rows)

    lanes = min(LANES, ndeg // 5)
    tiles = ndeg // lanes
    out = pl.pallas_call(
        functools.partial(update_kernel, nb),
        out_shape=jax.ShapeDtypeStruct((slots * nfld * tiles * 2, lanes), F32),
        in_specs=[smem, smem, anywhere, anywhere, anywhere],
        out_specs=anywhere,
        scratch_shapes=[
            pltpu.VMEM((nb, JPAD, LANES), BF16),
            pltpu.VMEM((slots, 2 * FPAD, ndeg), BF16),
            pltpu.VMEM((slots, nlat, ndeg), BF16),
            pltpu.VMEM((slots * nfld * tiles * 2, lanes), F32),
            pltpu.VMEM((FPAD, ndeg), F32),
            pltpu.VMEM((nb, JPAD, LANES), F32),
            pltpu.VMEM((nlat, LANES), F32),
            pltpu.VMEM((slots, 2 * FPAD, nlat), BF16),
            pltpu.SemaphoreType.DMA((1 + pairs,)),
            pltpu.SemaphoreType.DMA((pairs,)),
            pltpu.SemaphoreType.DMA((pairs,)),
        ],
        compiler_params=pltpu.CompilerParams(vmem_limit_bytes=56 * 1024 * 1024),
    )(slot_wave, mode_speed, arrived, values, leg_rows)
    out = out.reshape(slots, nfld, tiles, 2, lanes).transpose(0, 1, 3, 2, 4)
    return out.reshape(slots, nfld, 2, ndeg).transpose(0, 2, 1, 3)


def solution(mesh):
    return jax.shard_map(
        shards,
        mesh=mesh,
        in_specs=(P("band", None, "lev", None), P("band", None, None), P(), P(), P(), P(), P("lev")),
        out_specs=P("band", None, "lev", None),
        check_vma=False,
    )
```
